32 devices in a mesh: grp: 2 (over x), seq: 4 (over y, core), head: 4 (over z).
Axes of the slice: x: 2, y: 2, z: 4, core: 2. Of those that a mesh axis runs over, the one named last changes fastest.
Arguments:
- queries: bfloat16 [256, 4096], P(('grp', 'seq'), 'head'), parts along dimension 0, may hold values from -6 to 6
- root_keys: bfloat16 [8192, 4096], P(('grp', 'seq'), 'head'), parts along dimension 0, may hold values from -6 to 6
- root_values: bfloat16 [8192, 4096], P(('grp', 'seq'), 'head'), parts along dimension 0, may hold values from -6 to 6
- branch_keys: bfloat16 [8192, 4096], P(('grp', 'seq'), 'head'), parts along dimension 0, may hold values from -6 to 6
- branch_values: bfloat16 [8192, 4096], P(('grp', 'seq'), 'head'), parts along dimension 0, may hold values from -6 to 6
- branch_lengths: int32 [8], P(('grp', 'seq')), parts along dimension 0, may hold values from 1 to 1024, 2560 in all
- branch_ids: int32 [256], P('grp'), parts along dimension 0, may hold values from 0 to 3
- slopes: float32 [32], P('head'), may hold values from 0.0001953125 to 0.08
Outputs:
- attended: bfloat16 [256, 4096], P(('grp', 'seq'), 'head'), parts along dimension 0
The draws below stay inside these ranges and needn't reach their ends.
There are 2 independent parts, one for each index of `grp`. The reference program is written for one: setup_inputs(seed, part) draws one part's arguments, and reference() takes and returns one part's arrays. A program takes and returns all parts, laid end to end along the dimension named above; an argument that names none is the same for every part. Nothing has to cross between parts.
Inputs may be any that keep to these rules, and one draw needn't show every extreme that they name: `branch_lengths`: the longest branch holds exactly 1024 live positions; each holds at least one.
All inputs are finite; a program needn't handle non-finite values. No bound on the sum of `branch_lengths` on one device may be relied on, other than what follows from the above.
Results may differ from the reference program's by a relative error of at most 0.0041.
Values may be sent and summed in bfloat16 or wider, within the bound.
A program may use at most 128 MiB of HBM per device.

```python
import math
import jax
import jax.numpy as jnp
import numpy as np
from jax import lax

HEADS = 32
HEAD_DIM = 128
WIDTH = 4096
QROWS = 128
ROOT_DEV = 1024
ROOT = 4096
BRANCH = 1024
NBR = 4


def draw_queries(key, part):
    base = jnp.clip(jax.random.normal(jax.random.fold_in(key, 1), (QROWS, WIDTH), jnp.float32), -6.0, 6.0)
    return base.astype(jnp.bfloat16)


def draw_root_keys(key, part):
    base = jnp.clip(jax.random.normal(jax.random.fold_in(key, 2), (ROOT, WIDTH), jnp.float32), -6.0, 6.0)
    return base.astype(jnp.bfloat16)


def place_ends(values, key, low, high):
    extent = values.shape
    spot = [jax.random.randint(jax.random.fold_in(key, axis), (), 0, extent[axis]) for axis in range(len(extent))]
    values = values.at[tuple(spot)].set(low)
    longest = extent.index(max(extent))
    spot[longest] = (spot[longest] + 1) % extent[longest]
    return values.at[tuple(spot)].set(high)


def block_scale(rng, shape, cuts, least, largest):
    level = 1.0
    for dim, shards_of in cuts:
        draws = jax.random.uniform(jax.random.fold_in(jax.random.fold_in(rng, 6), dim), (shards_of,), jnp.float32, least / len(cuts), largest / len(cuts))
        level = level * jnp.repeat(jnp.exp(draws), shape[dim] // shards_of).reshape((-1,) + (1,) * (len(shape) - 1 - dim))
    return level


def split_up(count, total, most, lean):
    weights = [(1 << 20) // math.isqrt(rank ** lean) + 1 for rank in range(2, count + 1)]
    rest, counts = total - most - (count - 1), [1] * (count - 1)
    while rest > 0:
        candidates = [i for i in range(count - 1) if counts[i] < most]
        mass, left = sum([weights[i] for i in candidates]), rest
        for i in candidates:
            more = min(most - counts[i], max(1, left * weights[i] // mass), rest)
            counts[i] = counts[i] + more
            rest = rest - more
    return np.array([most] + counts)


def uneven(rng, amount, total, most, lean):
    if amount == 2:
        one = jax.random.randint(rng, (), max(1, total - most), min(most, total - 1) + 1)
        return jnp.stack([one, total - one])
    lengths = jnp.asarray(split_up(amount, total, most, lean), jnp.int32)
    twos = (amount - 1) // 2
    donor, taker = lengths[1:1 + 2 * twos:2], lengths[2:2 + 2 * twos:2]
    margin = jnp.minimum(donor - 1, most - taker)
    passed = jax.random.randint(jax.random.fold_in(rng, 1), (twos,), 0, 1 << 20) % (margin + 1)
    lengths = lengths.at[1:1 + 2 * twos:2].set(donor - passed).at[2:2 + 2 * twos:2].set(taker + passed)
    return lengths[jax.random.permutation(jax.random.fold_in(rng, 2), amount)]


def gaussian(rng, extent, deviation, limit, split=(), held_as=jnp.bfloat16):
    entries = jax.random.normal(rng, extent, jnp.float32) * deviation
    if len(split) > 0:
        entries = block_scale(rng, extent, split, -0.22, 0.18) * entries
    return jnp.clip(entries, min=-limit, max=limit).astype(held_as)


def setup_inputs(seed: int = 0, part: int = 0) -> dict:
    arg_keys = jax.random.split(jax.random.key(seed), 9)
    own_keys = jax.random.split(jax.random.fold_in(arg_keys[8], part), 9)
    return {
        "queries": draw_queries(jax.random.fold_in(jax.random.fold_in(arg_keys[8], part), 71), part),
        "root_keys": draw_root_keys(jax.random.fold_in(jax.random.fold_in(arg_keys[8], part), 71), part),
        "root_values": gaussian(own_keys[2], (ROOT, WIDTH), 1.0, 6.0, ((0, 4), (1, 4))),
        "branch_keys": gaussian(own_keys[3], (NBR * BRANCH, WIDTH), 1.0, 6.0, ((0, 4), (1, 4))),
        "branch_values": gaussian(own_keys[4], (NBR * BRANCH, WIDTH), 1.0, 6.0, ((0, 4), (1, 4))),
        "branch_lengths": uneven(own_keys[5], NBR, NBR * BRANCH * 5 // 8, BRANCH, 2).astype(jnp.int32),
        "branch_ids": place_ends(jax.random.randint(own_keys[6], (QROWS,), 0, NBR), jax.random.fold_in(own_keys[6], 1), 0, NBR - 1).astype(jnp.int32),
        "slopes": jnp.clip(jnp.exp(math.log(0.08) - 6.015181 * jax.random.uniform(arg_keys[7], (HEADS,), jnp.float32) ** block_scale(arg_keys[7], (HEADS,), ((0, 4),), -0.2, 0.2)), 0.0001953125, 0.08),
    }


def reference(queries, root_keys, root_values, branch_keys, branch_values, branch_lengths, branch_ids, slopes):
    scale = 1.0 / (HEAD_DIM ** 0.5)
    query_heads = jnp.transpose(queries.reshape(QROWS, HEADS, HEAD_DIM), (1, 0, 2))
    rkey_heads = jnp.transpose(root_keys.reshape(ROOT, HEADS, HEAD_DIM), (1, 0, 2))
    rval_heads = jnp.transpose(root_values.reshape(ROOT, HEADS, HEAD_DIM), (1, 0, 2))
    bkey_heads = jnp.transpose(branch_keys.reshape(NBR * BRANCH, HEADS, HEAD_DIM), (1, 0, 2))
    bval_heads = jnp.transpose(branch_values.reshape(NBR * BRANCH, HEADS, HEAD_DIM), (1, 0, 2))
    root_pos = jnp.arange(ROOT).astype(jnp.float32) - (ROOT + BRANCH)
    slot = jnp.arange(NBR * BRANCH)
    owner = (slot // BRANCH).astype(jnp.int32)
    offset = slot % BRANCH
    live = offset < branch_lengths[owner]
    match = (branch_ids[:, None] == owner[None, :]) & live[None, :]
    branch_pos = offset.astype(jnp.float32) - BRANCH
    dims = (((1,), (1,)), ((), ()))

    def one_head(items):
        query, rkey, rval, bkey, bval, slope = items
        scores = lax.dot_general(query, rkey, dims, preferred_element_type=jnp.float32) * scale + slope * root_pos[None, :]
        scores = scores.reshape(QROWS, NBR, ROOT_DEV)
        top_root = jnp.max(scores, axis=2)
        weights = jnp.exp(scores - top_root[:, :, None])
        total_root = jnp.sum(weights, axis=2)
        rounded = lax.optimization_barrier(weights.astype(jnp.bfloat16)).astype(jnp.float32)
        values = rval.astype(jnp.float32).reshape(NBR, ROOT_DEV, HEAD_DIM)
        out_root = jnp.einsum('qjk,jkd->qjd', rounded, values)
        bscores = lax.dot_general(query, bkey, dims, preferred_element_type=jnp.float32) * scale + slope * branch_pos[None, :]
        top_branch = jnp.max(jnp.where(match, bscores, -jnp.inf), axis=1)
        bweights = jnp.where(match, jnp.exp(bscores - top_branch[:, None]), 0.0)
        total_branch = jnp.sum(bweights, axis=1)
        out_branch = jnp.dot(bweights.astype(jnp.bfloat16), bval, preferred_element_type=jnp.float32)
        top = jnp.maximum(jnp.max(top_root, axis=1), top_branch)
        factor_root = jnp.exp(top_root - top[:, None])
        factor_branch = jnp.exp(top_branch - top)
        numer = jnp.sum(factor_root[:, :, None] * out_root, axis=1) + factor_branch[:, None] * out_branch
        denom = jnp.sum(factor_root * total_root, axis=1) + factor_branch * total_branch
        return numer / denom[:, None]

    result = lax.map(one_head, (query_heads, rkey_heads, rval_heads, bkey_heads, bval_heads, slopes))
    return jnp.transpose(result, (1, 0, 2)).reshape(QROWS, WIDTH).astype(jnp.bfloat16)
```

```python
import functools

import jax
import jax.numpy as jnp
from jax import lax
from jax.experimental import pallas as pl
from jax.experimental.pallas import tpu as pltpu
from jax.sharding import PartitionSpec as P

MESH = pl.DeviceIdType.MESH
LOG2E = 1.4426950408889634
MASKED = -1e30
LANES = 128
BLOCK = 2048
mark = jax.named_scope


def group_starts(heads):
    starts = [0, 1]
    while starts[-1] < heads:
        starts.append(min(2 * starts[-1], heads))
    return starts


def kernel(
    n,
    q_hbm,
    rk_hbm,
    rv_hbm,
    bk_hbm,
    bv_hbm,
    len_hbm,
    ids_hbm,
    slope_hbm,
    out_ref,
    len_ref,
    ids_ref,
    slope_ref,
    small_sem,
    kv,
    kaug,
    qaug,
    q_all,
    s_buf,
    o_send,
    o_recv,
    st_cols,
    st_send,
    st_recv,
    share_buf,
    kv_sem,
    own_sem,
    q_ssem,
    q_rsem,
    o_ssem,
    o_rsem,
    st_ssem,
    st_rsem,
):
    heads = slope_hbm.shape[0]
    query_dev = q_hbm.shape[0]
    rows = q_all.shape[0]
    root_dev = rk_hbm.shape[0]
    branch_len = bk_hbm.shape[0]
    keys = root_dev + branch_len
    size = q_hbm.shape[1] // heads
    scale = 1.0 / size**0.5
    rate = scale * LOG2E
    me = lax.axis_index("seq")
    peers = [(d, lax.rem(me + d, n)) for d in range(1, n)]
    mine = pl.ds(pl.multiple_of(me * query_dev, query_dev), query_dev)

    starts = group_starts(heads)

    def cols(h):
        return pl.ds(h * size, size)

    def group_of(h):
        return max(g for g in range(len(starts) - 1) if starts[g] <= h)

    def span_of(g):
        return pl.ds(starts[g] * size, (starts[g + 1] - starts[g]) * size)

    def fetch(which, h):
        source = (rk_hbm, bk_hbm, rv_hbm, bv_hbm)[which]
        span = (pl.ds(0, root_dev), pl.ds(root_dev, branch_len))[which % 2]
        return pltpu.make_async_copy(
            source.at[:, cols(h)], kv.at[h, which // 2, span], kv_sem.at[group_of(h)]
        )

    def fetched(g):
        some = kv.at[pl.ds(starts[g], starts[g + 1] - starts[g])]
        return pltpu.make_async_copy(some, some, kv_sem.at[g])

    own_copy = pltpu.make_async_copy(q_hbm, q_all.at[mine], own_sem.at[0])

    def q_copy(g, peer):
        part = q_all.at[mine, span_of(g)]
        return pltpu.make_async_remote_copy(
            src_ref=part,
            dst_ref=part,
            send_sem=q_ssem.at[0],
            recv_sem=q_rsem.at[g],
            device_id={"seq": peer},
            device_id_type=MESH,
        )

    def q_arrived(g):
        part = q_all.at[pl.ds(0, rows - query_dev), span_of(g)]
        return pltpu.make_async_copy(part, part, q_rsem.at[g])

    def q_sent():
        part = q_all.at[pl.ds(0, rows - query_dev)]
        return pltpu.make_async_copy(part, part, q_ssem.at[0])

    def o_copy(h, d, peer):
        theirs = pl.ds(pl.multiple_of(peer * query_dev, query_dev), query_dev)
        return pltpu.make_async_remote_copy(
            src_ref=o_send.at[h, theirs],
            dst_ref=o_recv.at[d - 1, h],
            send_sem=o_ssem.at[0],
            recv_sem=o_rsem.at[0],
            device_id={"seq": peer},
            device_id_type=MESH,
        )

    def st_copy(d, peer):
        return pltpu.make_async_remote_copy(
            src_ref=st_send,
            dst_ref=st_recv.at[d - 1],
            send_sem=st_ssem.at[0],
            recv_sem=st_rsem.at[0],
            device_id={"seq": peer},
            device_id_type=MESH,
        )

    def drain(buffer, sem):
        return pltpu.make_async_copy(buffer, buffer, sem.at[0])

    barrier = pltpu.get_barrier_semaphore()
    for _, peer in peers:
        pl.semaphore_signal(barrier, inc=1, device_id={"seq": peer}, device_id_type=MESH)
    small = (
        pltpu.make_async_copy(len_hbm, len_ref, small_sem.at[0]),
        pltpu.make_async_copy(ids_hbm, ids_ref, small_sem.at[1]),
        pltpu.make_async_copy(slope_hbm, slope_ref, small_sem.at[2]),
    )
    own_copy.start()
    for copy in small:
        copy.start()
    own_copy.wait()
    for copy in small:
        copy.wait()
    for h in range(heads):
        for which in range(4):
            fetch(which, h).start()
    with mark("P_barrier"):
        pl.semaphore_wait(barrier, n - 1)
    with mark("P_qissue"):
        for g in range(len(starts) - 1):
            for _, peer in peers:
                q_copy(g, peer).start()

    span = root_dev * n + branch_len

    @pl.loop(0, keys // LANES)
    def _(i):
        start = pl.multiple_of(i * LANES, LANES)
        spot = start + lax.broadcasted_iota(jnp.int32, (LANES, LANES), 0)
        lane = lax.broadcasted_iota(jnp.int32, (LANES, LANES), 1)
        is_branch = spot >= root_dev
        back = jnp.where(is_branch, keys - spot, span - me * root_dev - spot)
        low = back & 255
        dead = is_branch & (spot - root_dev >= len_ref[0])
        aug = jnp.where(
            lane < 6,
            jnp.where(lane < 3, low - back, -low).astype(jnp.float32),
            jnp.where(
                lane == 6,
                jnp.where(dead, MASKED, 0.0),
                jnp.where((lane == 7) & is_branch, 1.0, 0.0),
            ),
        )
        kaug[pl.ds(start, LANES), :] = aug.astype(jnp.bfloat16)

    down = lax.broadcasted_iota(jnp.int32, (rows, rows), 0)
    across = lax.broadcasted_iota(jnp.int32, (rows, rows), 1)
    other = jnp.where(ids_ref[...] == me, 0.0, MASKED)
    row_mask = jnp.sum(jnp.where(down == across, other, 0.0), axis=1, keepdims=True)
    qlane = lax.broadcasted_iota(jnp.int32, (rows, LANES), 1)
    qaug[...] = jnp.where(qlane == 6, 1.0, jnp.where(qlane == 7, row_mask, 0.0))
    st_cols[...] = jnp.zeros_like(st_cols)

    def await_head(h):
        if h in starts:
            fetched(starts.index(h)).wait()
            q_arrived(starts.index(h)).wait()

    def widened(h):
        slope = jnp.full((1, LANES), slope_ref[h] * (size**0.5), jnp.float32)
        first = slope.astype(jnp.bfloat16).astype(jnp.float32)
        second = (slope - first).astype(jnp.bfloat16).astype(jnp.float32)
        third = slope - first - second
        nth = lax.rem(lax.broadcasted_iota(jnp.int32, (1, LANES), 1), 3)
        parts = jnp.where(nth == 0, first, jnp.where(nth == 1, second, third))
        extra = jnp.where(qlane < 6, parts, qaug[...]).astype(jnp.bfloat16)
        return jnp.concatenate([q_all[:, cols(h)], extra], axis=1)

    def folded(combine, array):
        return functools.reduce(
            combine, [array[:, i : i + LANES] for i in range(0, array.shape[1], LANES)]
        )

    block = min(BLOCK, keys)

    def step(h_score, h_mix, top):
        query = None if h_score is None else widened(h_score)
        new_top, mixed, total = None, None, None
        for j in range(keys // block):
            at = pl.ds(j * block, block)
            if h_score is not None:
                key = jnp.concatenate([kv[h_score, 0, at], kaug[at]], axis=1)
                scores = lax.dot_general(
                    query, key, (((1,), (1,)), ((), ())), preferred_element_type=jnp.float32
                )
                s_buf[h_score % 2, :, at] = scores
                high = folded(jnp.maximum, scores)
                new_top = high if new_top is None else jnp.maximum(new_top, high)
            if h_mix is not None:
                weights = jnp.exp2((s_buf[h_mix % 2, :, at] - top) * rate)
                part = folded(jnp.add, weights)
                share = jnp.dot(
                    weights.astype(jnp.bfloat16),
                    kv[h_mix, 1, at],
                    preferred_element_type=jnp.float32,
                )
                mixed = share if mixed is None else mixed + share
                total = part if total is None else total + part
        if h_mix is not None:
            total = jnp.sum(total, axis=1, keepdims=True)
            level = top * rate + jnp.log(total) * LOG2E
            st_cols[...] = jnp.where(qlane == h_mix, level, st_cols[...])
            if h_mix + 1 == heads:
                st_send[...] = jnp.transpose(st_cols[...])[: st_send.shape[0]]
                for d, peer in peers:
                    st_copy(d, peer).start()
            o_send[h_mix] = (mixed / total).astype(jnp.bfloat16)
        if new_top is not None:
            return jnp.max(new_top, axis=1, keepdims=True)

    with mark("P_ak0"):
        await_head(0)
    with mark("P_s0"):
        top = step(0, None, None)
    for h in range(heads):
        last = h + 1 == heads
        if not last:
            with mark("P_ak%d" % (h + 1)):
                await_head(h + 1)
        with mark("P_step%d" % h):
            top = step(None if last else h + 1, h, top)
        for d, peer in peers:
            o_copy(h, d, peer).start()
    q_sent().wait()
    with mark("P_st"):
        drain(st_recv, st_rsem).wait()
    levels = [st_send[...]] + [st_recv[d - 1] for d, _ in peers]
    high = functools.reduce(jnp.maximum, levels)
    shares = [jnp.exp2(level - high) for level in levels]
    whole = functools.reduce(jnp.add, shares)
    deep = st_send.shape[0]
    blank = [jnp.zeros_like(whole)] * (-n % (LANES // deep))
    columns = jnp.concatenate([share / whole for share in shares] + blank, axis=0)
    share_buf[...] = jnp.transpose(columns)
    share = share_buf[mine]
    with mark('P_orecv'):
        drain(o_recv, o_rsem).wait()
    for h in range(heads):
        total = share[:, h : h + 1] * o_send[h, mine].astype(jnp.float32)
        for d, _ in peers:
            spot = d * deep + h
            total += share[:, spot : spot + 1] * o_recv[d - 1, h].astype(jnp.float32)
        out_ref[:, cols(h)] = total.astype(out_ref.dtype)
    with mark('P_osend'):
        drain(o_recv, o_ssem).wait()
        drain(st_recv, st_ssem).wait()


def shards(
    queries, root_keys, root_values, branch_keys, branch_values, branch_lengths, branch_ids, slopes
):
    n = lax.axis_size("seq")
    heads = slopes.shape[0]
    query_dev, width = queries.shape
    size = width // heads
    rows = branch_ids.shape[0]
    keys = root_keys.shape[0] + branch_keys.shape[0]
    deep = -(-heads // 8) * 8
    groups = len(group_starts(heads)) - 1
    hbm = pl.BlockSpec(memory_space=pl.ANY)
    vmem = pl.BlockSpec(memory_space=pltpu.VMEM)
    dma = pltpu.SemaphoreType.DMA
    return pl.pallas_call(
        functools.partial(kernel, n),
        out_shape=pltpu.VMEM((query_dev, width), jnp.bfloat16),
        in_specs=[hbm] * 8,
        out_specs=vmem,
        scratch_shapes=[
            pltpu.SMEM((1,), jnp.int32),
            pltpu.VMEM((1, rows), jnp.int32),
            pltpu.SMEM((heads,), jnp.float32),
            dma((3,)),
            pltpu.VMEM((heads, 2, keys, size), jnp.bfloat16),
            pltpu.VMEM((keys, LANES), jnp.bfloat16),
            pltpu.VMEM((rows, LANES), jnp.float32),
            pltpu.VMEM((rows, width), jnp.bfloat16),
            pltpu.VMEM((2, rows, keys), jnp.float32),
            pltpu.VMEM((heads, rows, size), jnp.bfloat16),
            pltpu.VMEM((n - 1, heads, query_dev, size), jnp.bfloat16),
            pltpu.VMEM((rows, LANES), jnp.float32),
            pltpu.VMEM((deep, rows), jnp.float32),
            pltpu.VMEM((n - 1, deep, rows), jnp.float32),
            pltpu.VMEM((rows, -(-n * deep // LANES) * LANES), jnp.float32),
            dma((groups,)),
            dma((1,)),
            dma((1,)),
            dma((groups,)),
            dma((1,)),
            dma((1,)),
            dma((1,)),
            dma((1,)),
        ],
        compiler_params=pltpu.CompilerParams(
            collective_id=0, has_side_effects=True, vmem_limit_bytes=60000 * 1024
        ),
    )(
        queries,
        root_keys,
        root_values,
        branch_keys,
        branch_values,
        branch_lengths,
        branch_ids.reshape(1, rows),
        slopes,
    )


def solution(mesh):
    in_specs = (
        P(("grp", "seq"), "head"),
        P(("grp", "seq"), "head"),
        P(("grp", "seq"), "head"),
        P(("grp", "seq"), "head"),
        P(("grp", "seq"), "head"),
        P(("grp", "seq")),
        P("grp"),
        P("head"),
    )
    out_specs = P(("grp", "seq"), "head")
    return jax.shard_map(shards, mesh=mesh, in_specs=in_specs, out_specs=out_specs, check_vma=False)
```
